32 devices in a mesh: member: 4 (over y, x), grid: 8 (over z, core).
Axes of the slice: x: 2, y: 2, z: 4, core: 2. Of those that a mesh axis runs over, the one named last changes fastest.
Arguments:
- latent: bfloat16 [4, 16384, 1024], P('member', 'grid'), may hold values from -6 to 6
- w_in: bfloat16 [1024, 1024], P(('member', 'grid')), may hold values from -0.1875 to 0.1875
- b_in: float32 [1024], replicated, may hold values from -3 to 3
- w_out: bfloat16 [100, 1024], replicated, may hold values from -0.1875 to 0.1875
- b_out: float32 [100], replicated, may hold values from -3 to 3
- targets: float32 [100, 16384], P(None, 'grid'), may hold values from -6 to 6
- var_weight: float32 [100], replicated, may hold values from 0.5 to 5
- plan: int32 [3, 4], replicated, may hold values from 0 to 3, as said below
Outputs:
- loss: float32 [], replicated
- grad_latent: bfloat16 [4, 16384, 1024], P('member', 'grid')
- grad_w_in: float32 [1024, 1024], P(('member', 'grid'))
- grad_b_in: float32 [1024], replicated
- grad_w_out: float32 [100, 1024], replicated
- grad_b_out: float32 [100], replicated
The draws below stay inside these ranges and needn't reach their ends.
Inputs may be any that keep to these rules, and one draw needn't show every extreme that they name: `plan`: each row is a perfect pairing of the 4 members: no member is its own partner, the partner of a member's partner is the member, and no pair occurs in two rows.
All inputs are finite; a program needn't handle non-finite values.
Results may differ from the reference program's by a relative error of at most 0.0095.
Values may be sent and summed in bfloat16 or wider, within the bound.
A program may use at most 128 MiB of HBM per device.

```python
import math
import jax
import jax.numpy as jnp
from jax import lax

L = 1024
V = 100
ROUNDS = 3
MEMBERS = 4
POINTS = 16384


def draw_plan(key, part):
    first_key, second_key = jax.random.split(jax.random.fold_in(key, 7))
    relabel = jax.random.permutation(first_key, MEMBERS).astype(jnp.int32)
    chosen = jax.random.permutation(second_key, MEMBERS - 1)[:ROUNDS].astype(jnp.int32)
    labels = jnp.arange(MEMBERS, dtype=jnp.int32)[None, :]
    rounds = chosen[:, None]
    partner = (2 * rounds - labels) % (MEMBERS - 1)
    partner = jnp.where(labels == rounds, MEMBERS - 1, partner)
    partner = jnp.where(labels == MEMBERS - 1, rounds, partner)
    mapped = relabel[partner]
    table = jnp.zeros((ROUNDS, MEMBERS), jnp.int32).at[:, relabel].set(mapped)
    return table.astype(jnp.int32)


def levels(stream_key, extent, cuts, least, largest):
    factor_of = 1.0
    for dim, parts in cuts:
        steps = jax.random.uniform(jax.random.fold_in(jax.random.fold_in(stream_key, 6), dim), (parts,), jnp.float32, least / len(cuts), largest / len(cuts))
        factor_of = factor_of * jnp.repeat(jnp.exp(steps), extent[dim] // parts).reshape((-1,) + (1,) * (len(extent) - 1 - dim))
    return factor_of


def normal_values(own_key, extent, width, most, pieces=(), kind=jnp.bfloat16):
    level = levels(own_key, extent, pieces, -0.22, 0.18) if pieces else 1.0
    entries = jax.random.normal(own_key, extent, jnp.float32) * width * level
    return jnp.minimum(jnp.maximum(entries, -most), most).astype(kind)


def setup_inputs(seed: int = 0) -> dict:
    key_list = jax.random.split(jax.random.key(seed), 9)
    return {
        "latent": normal_values(key_list[0], (MEMBERS, POINTS, L), 1.0, 6.0, ((0, 4), (1, 8))),
        "w_in": normal_values(key_list[1], (L, L), L ** -0.5, 0.1875, ((0, 32),)),
        "b_in": normal_values(key_list[2], (L,), 0.5, 3.0, (), jnp.float32),
        "w_out": normal_values(key_list[3], (V, L), L ** -0.5, 0.1875),
        "b_out": normal_values(key_list[4], (V,), 0.5, 3.0, (), jnp.float32),
        "targets": normal_values(key_list[5], (V, POINTS), 1.0, 6.0, ((1, 8),), jnp.float32),
        "var_weight": jnp.clip(jnp.exp(jax.random.uniform(key_list[6], (V,), jnp.float32, math.log(0.5), math.log(5.0))), 0.5, 5.0),
        "plan": draw_plan(jax.random.fold_in(key_list[8], 71), 0),
    }


DELTA = 0.25

def reference(latent, w_in, b_in, w_out, b_out, targets, var_weight, plan):
    place = jnp.arange(POINTS).astype(jnp.float32)
    area = jnp.cos(1.4 * (place + 0.5) / POINTS)
    scale_map = area[None, :] * var_weight[:, None]

    def forward(hidden_in):
        pre = jnp.dot(hidden_in, w_in, preferred_element_type=jnp.float32) + b_in[None, :]
        act = jax.nn.gelu(pre).astype(jnp.bfloat16)
        field = jnp.dot(w_out, act.T, preferred_element_type=jnp.float32) + b_out[:, None]
        return field
    fields = lax.map(forward, latent)

    def member_step(carry, member):
        acc_w1, acc_w2, acc_b1, acc_b2, acc_loss = carry
        hidden_in = latent[member]
        field = fields[member]
        others = fields[plan[:, member]]
        diff = field[None] - others
        root = jnp.sqrt(diff * diff + DELTA * DELTA)
        pairs = lax.optimization_barrier(jnp.sum(diff / root, axis=0))
        spread = lax.optimization_barrier(jnp.sum(root - DELTA, axis=0))
        miss = field - targets
        miss_root = jnp.sqrt(miss * miss + DELTA * DELTA)
        cot = scale_map * (miss / miss_root - pairs / ROUNDS)
        terms = scale_map * (miss_root - DELTA - spread / (2.0 * ROUNDS))
        cot_b = cot.astype(jnp.bfloat16)
        pre = jnp.dot(hidden_in, w_in, preferred_element_type=jnp.float32) + b_in[None, :]
        act = jax.nn.gelu(pre).astype(jnp.bfloat16)
        dact = jnp.dot(cot_b.T, w_out, preferred_element_type=jnp.float32)
        _, pull = jax.vjp(jax.nn.gelu, pre)
        dpre = pull(dact)[0]
        dpre_b = dpre.astype(jnp.bfloat16)
        grad_hidden = jnp.dot(dpre_b, w_in.T, preferred_element_type=jnp.float32).astype(jnp.bfloat16)
        acc_w1 = acc_w1 + jnp.dot(hidden_in.T, dpre_b, preferred_element_type=jnp.float32)
        acc_w2 = acc_w2 + jnp.dot(cot_b, act, preferred_element_type=jnp.float32)
        acc_b1 = acc_b1 + lax.optimization_barrier(jnp.sum(dpre, axis=0))
        acc_b2 = acc_b2 + lax.optimization_barrier(jnp.sum(cot, axis=1))
        acc_loss = acc_loss + jnp.sum(terms)
        return ((acc_w1, acc_w2, acc_b1, acc_b2, acc_loss), grad_hidden)
    start = (jnp.zeros((L, L), jnp.float32), jnp.zeros((V, L), jnp.float32), jnp.zeros((L,), jnp.float32), jnp.zeros((V,), jnp.float32), jnp.zeros((), jnp.float32))
    (acc_w1, acc_w2, acc_b1, acc_b2, acc_loss), grad_latent = lax.scan(member_step, start, jnp.arange(MEMBERS).astype(jnp.int32))
    kappa = 4.0 / jnp.sqrt(jnp.float32(MEMBERS * POINTS))
    loss = acc_loss / (MEMBERS * POINTS * V)
    return (loss, grad_latent, acc_w1 * kappa, acc_b1 * kappa, acc_w2 * kappa, acc_b2 * kappa)
```

```python
import functools
import math

import jax
import jax.numpy as jnp
from jax import lax
from jax.experimental import pallas as pl
from jax.experimental.pallas import tpu as pltpu
from jax.sharding import PartitionSpec as P

DELTA = 0.25


def make_fold(mine, partner_rows):

    def fold(carry, piece, start):
        count = piece.shape[0]
        labels = jnp.arange(count, dtype=jnp.int32)
        weights = jnp.sum((partner_rows[:, None] == labels[None, :]).astype(jnp.float32), axis=0)
        diff = mine[None] - piece
        root = jnp.sqrt(diff * diff + DELTA * DELTA)
        slope_sum = jnp.einsum("k,kvp->vp", weights, diff / root)
        spread_sum = jnp.einsum("k,kvp->vp", weights, root - DELTA)
        return (slope_sum, spread_sum)

    return fold


def shards(latent, w_in, b_in, w_out, b_out, targets, var_weight, plan):
    hidden_in = latent[0]
    points = hidden_in.shape[0]
    rounds = plan.shape[0]
    w_full = lax.all_gather(w_in, ("member", "grid"), axis=0, tiled=True)
    member = lax.axis_index("member")
    grid_index = lax.axis_index("grid")
    members = lax.axis_size("member")
    grid_count = lax.axis_size("grid")
    total = points * grid_count
    place = (grid_index * points + jnp.arange(points, dtype=jnp.int32)).astype(jnp.float32)
    area = jnp.cos(1.4 * (place + 0.5) / total)
    scale_map = area[None, :] * var_weight[:, None]
    partner_rows = lax.dynamic_index_in_dim(plan, member, 1, keepdims=False)
    pre = jnp.dot(hidden_in, w_full, preferred_element_type=jnp.float32) + b_in[None, :]
    act = jax.nn.gelu(pre).astype(jnp.bfloat16)
    field = jnp.dot(w_out, act.T, preferred_element_type=jnp.float32) + b_out[:, None]
    pre, act, field = (pre, act, field)
    fold_all = make_fold(field, partner_rows)
    slope_sum, spread_sum = fold_all(
        (
            jnp.zeros((w_out.shape[0], points), jnp.float32),
            jnp.zeros((w_out.shape[0], points), jnp.float32),
        ),
        lax.all_gather(field[None], "member", axis=0, tiled=True),
        jnp.int32(0),
    )
    miss = field - targets
    miss_root = jnp.sqrt(miss * miss + DELTA * DELTA)
    cot = scale_map * (miss / miss_root - slope_sum / rounds)
    terms = scale_map * (miss_root - DELTA - spread_sum / (2.0 * rounds))
    cot_b = cot.astype(jnp.bfloat16)
    dact = jnp.dot(cot_b.T, w_out, preferred_element_type=jnp.float32)
    _, pull = jax.vjp(jax.nn.gelu, pre)
    dpre = pull(dact)[0]
    dpre_b = dpre.astype(jnp.bfloat16)
    grad_hidden = jnp.dot(dpre_b, w_full.T, preferred_element_type=jnp.float32).astype(jnp.bfloat16)
    kappa = 4.0 / jnp.sqrt(jnp.float32(members * total))
    out_term = jnp.dot(cot_b, act, preferred_element_type=jnp.float32)
    sum_w2, sum_b2, sum_b1, sum_loss = lax.psum(
        (out_term, jnp.sum(cot, axis=1), jnp.sum(dpre, axis=0), jnp.sum(terms)), ("member", "grid")
    )
    row_count = w_in.shape[0]
    full_term = jnp.dot(hidden_in.T, dpre_b, preferred_element_type=jnp.float32)
    summed = lax.psum(full_term, ("member", "grid"))
    offset = (member * grid_count + grid_index) * row_count
    own_rows = lax.dynamic_slice_in_dim(summed, offset, row_count, 0)
    loss = sum_loss / (members * total * w_out.shape[0])
    return (
        loss,
        grad_hidden[None],
        own_rows * kappa,
        sum_b1 * kappa,
        sum_w2 * kappa,
        sum_b2 * kappa,
    )


TILE = 256
LANES = 128
BF = jnp.bfloat16
F32 = jnp.float32


def dot(a, b, dims):
    return lax.dot_general(a, b, (dims, ((), ())), preferred_element_type=F32)


NN = ((1,), (0,))
NT = ((1,), (1,))
TN = ((0,), (0,))


def head_kernel(
    members, planes, lat_hbm, w_in, b_in, w_out, b_out, tgt_hbm, vw,
    gh_hbm, g_w1, g_b1, g_w2, g_b2, g_loss,
    lat, lat_t, w_buf, gp, act, dpre, gh, fsend, frecv, csend, crecv, tgt, rowbuf, lane_sums,
    ot, op_send, op_recv, om_keep, om_send, om_recv, oz, w2, sm, sp_recv, smm, smz,
    keep, p_send, p_recv, m_send, m_recv, z_keep, z_send, z_recv,
    send_sem, recv_sem, local_sem, out_sem,
):
    m = lax.axis_index("member")
    g = lax.axis_index("grid")
    z, c = g // 2, lax.rem(g, 2)
    other = 1 - c
    points = lat.shape[1]
    width = lat.shape[2]
    sub = points // members
    rows = w_in.shape[0]
    vars_ = w_out.shape[0]
    latent = w_out.shape[1]
    total = points * planes * 2

    def mem(k):
        return lax.rem(m + k + members, members)

    def zed(k):
        return lax.rem(z + k + planes, planes)

    partner = (m, z * 2 + other)

    def member_dev(k):
        return (mem(k), g)

    def z_dev(k):
        return (m, zed(k) * 2 + c)

    started = []

    def send(src, dst, dev):
        n = len(started)
        copy = pltpu.make_async_remote_copy(
            src_ref=src, dst_ref=dst, send_sem=send_sem.at[n], recv_sem=recv_sem.at[n],
            device_id=dev, device_id_type=pl.DeviceIdType.MESH,
        )
        copy.start()
        started.append(copy)
        return copy

    loads = []
    for ch in range(members):
        copy = pltpu.make_async_copy(
            lat_hbm.at[0, :, pl.ds(ch * width, width)], lat.at[ch], local_sem.at[ch]
        )
        copy.start()
        loads.append(copy)
    own = pltpu.make_async_copy(w_in, w_buf.at[m, z, c], local_sem.at[members])
    own.start()
    tgt_copy = pltpu.make_async_copy(
        tgt_hbm.at[:, pl.ds(pl.multiple_of(m * sub, LANES), sub)], tgt, local_sem.at[members + 1]
    )
    tgt_copy.start()

    barrier = pltpu.get_barrier_semaphore()
    peers = [partner] + [z_dev(k) for k in range(1, planes)] + [member_dev(k) for k in range(1, members)]
    for dev in peers:
        pl.semaphore_signal(barrier, inc=1, device_id=dev, device_id_type=pl.DeviceIdType.MESH)
    pl.semaphore_wait(barrier, len(peers))

    z_copies = [send(w_in, w_buf.at[m, z, c], z_dev(k)) for k in range(1, planes)]

    for copy in loads:
        copy.wait()
    own.wait()
    for copy in z_copies:
        copy.wait_recv()
    half = w_buf.at[m, :, c]
    mem_copies = [None] + [send(half, half, member_dev(k)) for k in range(1, members)]
    part_copies = [send(half, half, partner)]

    def transpose_chunk(ch):
        def body(t, carry):
            r0 = pl.multiple_of(t * TILE, TILE)
            lat_t[ch, :, pl.ds(r0, TILE)] = lat[ch, pl.ds(r0, TILE), :].T
            return carry
        lax.fori_loop(0, points // TILE, body, 0)

    for ch in range(members):
        transpose_chunk(ch)
    rowbuf[...] = jnp.zeros_like(rowbuf)
    rowbuf[0:1, :vars_] = b_out[...]
    rowbuf[1:2, :vars_] = vw[...]
    b_col = jnp.broadcast_to(rowbuf[0:1, :], (LANES, LANES)).T[:vars_]
    v_col = jnp.broadcast_to(rowbuf[1:2, :], (LANES, LANES)).T[:vars_]
    lane_sums[...] = jnp.zeros_like(lane_sums)
    ot[...] = jnp.zeros_like(ot)
    sm[...] = jnp.zeros_like(sm)

    for k in range(members):
        ch = mem(-k)
        if k > 0:
            mem_copies[k].wait_recv()
            got = w_buf.at[ch, :, c]
            part_copies.append(send(got, got, partner))
        part_copies[k].wait_recv()
        if k == members - 1:
            break

        def body(t, carry, ch=ch, first=k == 0):
            r0 = pl.multiple_of(t * TILE, TILE)
            w = w_buf[ch].reshape(width, latent)
            before = b_in[...] if first else gp[pl.ds(r0, TILE), :]
            gp[pl.ds(r0, TILE), :] = before + dot(lat[ch, pl.ds(r0, TILE), :], w, NN)
            return carry

        lax.fori_loop(0, points // TILE, body, 0)

    last = mem(1 - members)
    c0 = math.sqrt(2.0 / math.pi)
    f_copies = [None]
    for k in range(1, members + 1):
        base = mem(k) * sub

        def body(t, carry, base=base):
            r0 = pl.multiple_of(base + t * TILE, TILE)
            x = dot(lat[last, pl.ds(r0, TILE), :], w_buf[last].reshape(width, latent), NN)
            x = x + (b_in[...] if members == 1 else gp[pl.ds(r0, TILE), :])
            sq = x * x
            th = jnp.tanh(c0 * x * (1.0 + 0.044715 * sq))
            cdf = 0.5 + 0.5 * th
            act[pl.ds(r0, TILE), :] = (x * cdf).astype(BF)
            gp[pl.ds(r0, TILE), :] = cdf + 0.5 * x * (1.0 - th * th) * (c0 + (3.0 * 0.044715 * c0) * sq)
            return carry

        lax.fori_loop(0, sub // TILE, body, 0)
        field = dot(w_out[...], act[pl.ds(pl.multiple_of(base, TILE), sub), :], NT)
        if k < members:
            fsend[k - 1] = field
            f_copies.append(send(fsend.at[k - 1], frecv.at[k], member_dev(k)))
        else:
            frecv[0] = field

    tgt_copy.wait()
    for k in range(1, members):
        f_copies[k].wait_recv()
    eps = DELTA * DELTA
    b_sum = jnp.zeros((vars_, LANES), F32)
    l_sum = jnp.zeros((vars_, LANES), F32)
    for t in range(sub // LANES):
        cols = slice(t * LANES, (t + 1) * LANES)
        place = lax.broadcasted_iota(jnp.int32, (1, LANES), 1) + (g * points + m * sub + t * LANES)
        area = jnp.cos(1.4 * (place.astype(F32) + 0.5) / total)
        scale = v_col * area
        f = [frecv[k, :, cols] for k in range(members)]
        goal = tgt[:, cols] - b_col
        pairs = [None] * members
        spread = jnp.zeros((vars_, LANES), F32)
        for a in range(members):
            for b in range(a + 1, members):
                d = f[a] - f[b]
                q = d * d + eps
                inv = lax.rsqrt(q)
                s = d * inv
                spread += q * inv - DELTA
                pairs[a] = s if pairs[a] is None else pairs[a] + s
                pairs[b] = -s if pairs[b] is None else pairs[b] - s
        miss_sum = jnp.zeros((vars_, LANES), F32)
        for a in range(members):
            d = f[a] - goal
            q = d * d + eps
            inv = lax.rsqrt(q)
            miss_sum += q * inv - DELTA
            cot = scale * (d * inv - pairs[a] * (1.0 / (members - 1)))
            b_sum += cot
            if a == 0:
                crecv[0, :, cols] = cot.astype(BF)
            else:
                csend[a - 1, :, cols] = cot.astype(BF)
        l_sum += scale * (miss_sum - spread * (1.0 / (members - 1)))
    c_copies = [None] + [send(csend.at[a - 1], crecv.at[a], member_dev(-a)) for a in range(1, members)]
    lane_sums[:vars_, :] = b_sum
    sm[1:2, :LANES] = jnp.sum(lane_sums[...].T, axis=0, keepdims=True)
    sm[1:2, LANES:2 * LANES] = jnp.sum(l_sum, axis=0, keepdims=True)

    col = jnp.zeros((1, latent), F32)
    for a in range(members):
        if a > 0:
            c_copies[a].wait_recv()
        base = mem(a) * sub

        def body(t, carry, base=base, a=a):
            r0 = pl.multiple_of(base + t * TILE, TILE)
            cot_b = crecv[a, :, pl.ds(pl.multiple_of(t * TILE, TILE), TILE)]
            d = dot(cot_b, w_out[...], TN) * gp[pl.ds(r0, TILE), :]
            dpre[pl.ds(r0, TILE), :] = d.astype(BF)
            ot[:vars_, :] += dot(cot_b, act[pl.ds(r0, TILE), :], NN)
            return carry + jnp.sum(d, axis=0, keepdims=True)

        col = lax.fori_loop(0, sub // TILE, body, col)
    sm[0:1, :] = col

    share = ot.shape[0] // (2 * members)
    first_half = pl.multiple_of(other * (members * share), share)
    op_send[...] = ot[pl.ds(first_half, members * share), :].astype(BF)
    op_copy = send(op_send, op_recv, partner)
    sp_copy = send(sm, sp_recv, partner)

    def chunk(k):
        t = mem(k)
        part = dot(lat_t[t], dpre[...], NN).reshape(planes, 2, rows, latent)
        gather_ref = keep
        gather_ref[...] = part
        p_send[k - 1] = keep[:, other].astype(BF)
        m_keep_k = keep[:, c]
        return m_keep_k, send(p_send.at[k - 1], p_recv.at[k - 1], partner)

    def chip_sum(k, mine, copy):
        copy.wait_recv()
        return mine + p_recv[k - 1].astype(F32)

    def to_member(k):
        p_copies[k].wait_recv()
        m_send[k - 1] = (z_keep[k - 1] + p_recv[k - 1].astype(F32)).astype(BF)
        return send(m_send.at[k - 1], m_recv.at[k - 1], member_dev(k))

    p_copies = {}
    m_copies = {}

    def do_chunk(k):
        mine, copy = chunk(k)
        z_keep[k - 1] = mine
        p_copies[k] = copy

    do_chunk(1)
    op_copy.wait_recv()
    mine = pl.multiple_of(c * (members * share), share)
    om_keep[...] = (ot[pl.ds(mine, members * share), :] + op_recv[...].astype(F32)).reshape(members, share, latent)
    om_send[...] = om_keep[...].astype(BF)
    om_copies = [send(om_send.at[mem(k)], om_recv.at[k - 1], member_dev(k)) for k in range(1, members)]
    sp_copy.wait_recv()
    smm[m] = sm[...] + sp_recv[...]
    sm_copies = [send(smm.at[m], smm.at[m], member_dev(k)) for k in range(1, members)]
    do_chunk(2)
    m_copies[1] = to_member(1)
    acc = om_keep[m]
    for k in range(1, members):
        om_copies[k - 1].wait_recv()
        acc += om_recv[k - 1].astype(F32)
    oz[z] = acc.astype(BF)
    oz_copies = [send(oz.at[z], oz.at[z], z_dev(k)) for k in range(1, planes)]
    for copy in sm_copies:
        copy.wait_recv()
    acc = smm[0]
    for k in range(1, members):
        acc += smm[k]
    smz[z] = acc
    sz_copies = [send(smz.at[z], smz.at[z], z_dev(k)) for k in range(1, planes)]
    for k in range(3, members):
        do_chunk(k)
        m_copies[k - 1] = to_member(k - 1)
    for copy in oz_copies:
        copy.wait_recv()
    acc = oz[0].astype(F32)
    for k in range(1, planes):
        acc += oz[k].astype(F32)
    w2[c, m] = acc
    w2_copies = [send(w2.at[c, m], w2.at[c, m], member_dev(k)) for k in range(1, members)]
    do_chunk(members)
    m_copies[members - 1] = to_member(members - 1)
    for copy in w2_copies:
        copy.wait_recv()
    half_copy = send(w2.at[c], w2.at[c], partner)

    outs = []
    for ch in range(members):
        def body(t, carry, ch=ch):
            r0 = pl.multiple_of(t * TILE, TILE)
            w = w_buf[ch].reshape(width, latent)
            gh[ch, pl.ds(r0, TILE), :] = dot(dpre[pl.ds(r0, TILE), :], w, NT).astype(BF)
            return carry

        lax.fori_loop(0, points // TILE, body, 0)
        copy = pltpu.make_async_copy(gh.at[ch], gh_hbm.at[0, :, pl.ds(ch * width, width)], out_sem.at[ch])
        copy.start()
        outs.append(copy)

    kappa = 4.0 / math.sqrt(members * total)
    p_copies[members].wait_recv()
    acc = z_keep[members - 1] + p_recv[members - 1].astype(F32)
    for k in range(1, members):
        m_copies[k].wait_recv()
        acc += m_recv[k - 1].astype(F32)
    z_keep[members - 1] = acc
    z_send[...] = acc.astype(BF)
    zz_copies = [send(z_send.at[zed(k)], z_recv.at[k - 1], z_dev(k)) for k in range(1, planes)]

    for copy in sz_copies:
        copy.wait_recv()
    acc = smz[0]
    for k in range(1, planes):
        acc += smz[k]
    acc = acc * kappa
    g_b1[...] = acc[0:1, :]
    g_b2[...] = acc[1:2, :vars_]
    g_loss[...] = jnp.sum(acc[1:2, LANES:2 * LANES], axis=1, keepdims=True) * (1.0 / (kappa * members * total * vars_))
    half_copy.wait_recv()
    g_w2[...] = w2[...].reshape(2 * members * share, latent)[:vars_] * kappa

    acc = z_keep[members - 1, z]
    for k in range(1, planes):
        zz_copies[k - 1].wait_recv()
        acc += z_recv[k - 1].astype(F32)
    g_w1[...] = acc * kappa
    for copy in started:
        copy.wait_send()
    for copy in outs:
        copy.wait()


def fast(latent, w_in, b_in, w_out, b_out, targets, var_weight, plan):
    members = lax.axis_size("member")
    grid = lax.axis_size("grid")
    planes = grid // 2
    points, width = latent.shape[1], latent.shape[2]
    rows = w_in.shape[0]
    vars_ = w_out.shape[0]
    sub = points // members
    cw = width // members
    share = 16 * pl.cdiv(vars_, 32 * members)
    n_sems = (planes - 1) * 4 + (members - 1) * 8 + 2 * members + 3
    vmem = pl.BlockSpec(memory_space=pltpu.VMEM)
    hbm = pl.BlockSpec(memory_space=pl.ANY)
    V = pltpu.VMEM
    scratch = [
        V((members, points, cw), BF), V((members, cw, points), BF), V((members, planes, 2, rows, width), BF),
        V((points, width), F32), V((points, width), BF), V((points, width), BF), V((members, points, cw), BF),
        V((members - 1, vars_, sub), F32), V((members, vars_, sub), F32),
        V((members - 1, vars_, sub), BF), V((members, vars_, sub), BF), V((vars_, sub), F32),
        V((8, LANES), F32), V((LANES, LANES), F32),
        V((2 * members * share, width), F32), V((members * share, width), BF), V((members * share, width), BF),
        V((members, share, width), F32), V((members, share, width), BF), V((members - 1, share, width), BF),
        V((planes, share, width), BF), V((2, members, share, width), F32),
        V((2, width), F32), V((2, width), F32), V((members, 2, width), F32), V((planes, 2, width), F32),
        V((planes, 2, rows, width), F32), V((members, planes, rows, width), BF), V((members, planes, rows, width), BF),
        V((members - 1, planes, rows, width), BF), V((members - 1, planes, rows, width), BF),
        V((members, planes, rows, width), F32), V((planes, rows, width), BF), V((planes - 1, rows, width), BF),
        pltpu.SemaphoreType.DMA((n_sems,)), pltpu.SemaphoreType.DMA((n_sems,)),
        pltpu.SemaphoreType.DMA((members + 2,)), pltpu.SemaphoreType.DMA((members,)),
    ]
    S = jax.ShapeDtypeStruct
    gh, g_w1, g_b1, g_w2, g_b2, g_loss = pl.pallas_call(
        functools.partial(head_kernel, members, planes),
        out_shape=[
            S((1, points, width), BF), S((rows, width), F32), S((1, width), F32),
            S((vars_, width), F32), S((1, vars_), F32), S((1, 1), F32),
        ],
        in_specs=[hbm, vmem, vmem, vmem, vmem, hbm, vmem],
        out_specs=[hbm, vmem, vmem, vmem, vmem, vmem],
        scratch_shapes=scratch,
        compiler_params=pltpu.CompilerParams(
            collective_id=0, has_side_effects=True, vmem_limit_bytes=60 * 1024 * 1024
        ),
    )(latent, w_in, b_in[None], w_out, b_out[None], targets, var_weight[None])
    return g_loss[0, 0], gh, g_w1, g_b1[0], g_w2, g_b2[0]


def local(latent, w_in, b_in, w_out, b_out, targets, var_weight, plan):
    members = lax.axis_size("member")
    grid = lax.axis_size("grid")
    points, width = latent.shape[1], latent.shape[2]
    whole_plan = plan.shape[0] == members - 1 and members >= 3
    tiled = (
        w_in.shape[0] % 16 == 0 and grid % 2 == 0 and grid >= 4
        and points % (members * TILE) == 0 and width % (members * LANES) == 0
        and width // members == grid * w_in.shape[0] and w_out.shape[0] <= LANES
        and points * width <= 2048 * 1024
    )
    run = fast if whole_plan and tiled else shards
    return run(latent, w_in, b_in, w_out, b_out, targets, var_weight, plan)


def solution(mesh):
    placed = (
        P("member", "grid", None),
        P(("member", "grid"), None),
        P(),
        P(),
        P(),
        P(None, "grid"),
        P(),
        P(),
    )
    return jax.shard_map(
        local,
        mesh=mesh,
        in_specs=placed,
        out_specs=(P(), P("member", "grid", None), P(("member", "grid"), None), P(), P(), P()),
        check_vma=False,
    )
```

```python
import functools
import math

import jax
import jax.numpy as jnp
from jax import lax
from jax.experimental import pallas as pl
from jax.experimental.pallas import tpu as pltpu
from jax.sharding import PartitionSpec as P

DELTA = 0.25


def make_fold(mine, partner_rows):

    def fold(carry, piece, start):
        count = piece.shape[0]
        labels = jnp.arange(count, dtype=jnp.int32)
        weights = jnp.sum((partner_rows[:, None] == labels[None, :]).astype(jnp.float32), axis=0)
        diff = mine[None] - piece
        root = jnp.sqrt(diff * diff + DELTA * DELTA)
        slope_sum = jnp.einsum("k,kvp->vp", weights, diff / root)
        spread_sum = jnp.einsum("k,kvp->vp", weights, root - DELTA)
        return (slope_sum, spread_sum)

    return fold


def shards(latent, w_in, b_in, w_out, b_out, targets, var_weight, plan):
    hidden_in = latent[0]
    points = hidden_in.shape[0]
    rounds = plan.shape[0]
    w_full = lax.all_gather(w_in, ("member", "grid"), axis=0, tiled=True)
    member = lax.axis_index("member")
    grid_index = lax.axis_index("grid")
    members = lax.axis_size("member")
    grid_count = lax.axis_size("grid")
    total = points * grid_count
    place = (grid_index * points + jnp.arange(points, dtype=jnp.int32)).astype(jnp.float32)
    area = jnp.cos(1.4 * (place + 0.5) / total)
    scale_map = area[None, :] * var_weight[:, None]
    partner_rows = lax.dynamic_index_in_dim(plan, member, 1, keepdims=False)
    pre = jnp.dot(hidden_in, w_full, preferred_element_type=jnp.float32) + b_in[None, :]
    act = jax.nn.gelu(pre).astype(jnp.bfloat16)
    field = jnp.dot(w_out, act.T, preferred_element_type=jnp.float32) + b_out[:, None]
    pre, act, field = (pre, act, field)
    fold_all = make_fold(field, partner_rows)
    slope_sum, spread_sum = fold_all(
        (
            jnp.zeros((w_out.shape[0], points), jnp.float32),
            jnp.zeros((w_out.shape[0], points), jnp.float32),
        ),
        lax.all_gather(field[None], "member", axis=0, tiled=True),
        jnp.int32(0),
    )
    miss = field - targets
    miss_root = jnp.sqrt(miss * miss + DELTA * DELTA)
    cot = scale_map * (miss / miss_root - slope_sum / rounds)
    terms = scale_map * (miss_root - DELTA - spread_sum / (2.0 * rounds))
    cot_b = cot.astype(jnp.bfloat16)
    dact = jnp.dot(cot_b.T, w_out, preferred_element_type=jnp.float32)
    _, pull = jax.vjp(jax.nn.gelu, pre)
    dpre = pull(dact)[0]
    dpre_b = dpre.astype(jnp.bfloat16)
    grad_hidden = jnp.dot(dpre_b, w_full.T, preferred_element_type=jnp.float32).astype(jnp.bfloat16)
    kappa = 4.0 / jnp.sqrt(jnp.float32(members * total))
    out_term = jnp.dot(cot_b, act, preferred_element_type=jnp.float32)
    sum_w2, sum_b2, sum_b1, sum_loss = lax.psum(
        (out_term, jnp.sum(cot, axis=1), jnp.sum(dpre, axis=0), jnp.sum(terms)), ("member", "grid")
    )
    row_count = w_in.shape[0]
    full_term = jnp.dot(hidden_in.T, dpre_b, preferred_element_type=jnp.float32)
    summed = lax.psum(full_term, ("member", "grid"))
    offset = (member * grid_count + grid_index) * row_count
    own_rows = lax.dynamic_slice_in_dim(summed, offset, row_count, 0)
    loss = sum_loss / (members * total * w_out.shape[0])
    return (
        loss,
        grad_hidden[None],
        own_rows * kappa,
        sum_b1 * kappa,
        sum_w2 * kappa,
        sum_b2 * kappa,
    )


TILE = 256
LANES = 128
BF = jnp.bfloat16
F32 = jnp.float32


def dot(a, b, dims):
    return lax.dot_general(a, b, (dims, ((), ())), preferred_element_type=F32)


NN = ((1,), (0,))
NT = ((1,), (1,))
TN = ((0,), (0,))


def head_kernel(
    members, planes, lat_hbm, w_in, b_in, w_out, b_out, tgt_hbm, vw,
    gh_hbm, g_w1, g_b1, g_w2, g_b2, g_loss,
    lat, lat_t, w_buf, gp, act, dpre, gh, fsend, frecv, csend, crecv, tgt, rowbuf, lane_sums,
    ot, op_send, op_recv, om_keep, om_send, om_recv, oz, w2, sm, sp_recv, smm, smz,
    keep, p_send, p_recv, m_send, m_recv, z_keep, z_send, z_recv,
    send_sem, recv_sem, local_sem, out_sem,
):
    m = lax.axis_index("member")
    g = lax.axis_index("grid")
    z, c = g // 2, lax.rem(g, 2)
    other = 1 - c
    points = lat.shape[1]
    width = lat.shape[2]
    sub = points // members
    rows = w_in.shape[0]
    vars_ = w_out.shape[0]
    latent = w_out.shape[1]
    total = points * planes * 2

    across, down = m + 1 - 2 * lax.rem(m, 2), m + 2 - 4 * (m // 2)
    order = (m, members - 1 - m, across, down)

    def mem(k):
        return order[k % members]

    def zed(k):
        return lax.rem(z + k + planes, planes)

    partner = (m, z * 2 + other)

    def member_dev(k):
        return (mem(k), g)

    def z_dev(k):
        return (m, zed(k) * 2 + c)

    started = []

    def send(src, dst, dev):
        n = len(started)
        copy = pltpu.make_async_remote_copy(
            src_ref=src, dst_ref=dst, send_sem=send_sem.at[n], recv_sem=recv_sem.at[n],
            device_id=dev, device_id_type=pl.DeviceIdType.MESH,
        )
        copy.start()
        started.append(copy)
        return copy

    loads = []
    for ch in range(members):
        copy = pltpu.make_async_copy(
            lat_hbm.at[0, :, pl.ds(ch * width, width)], lat.at[ch], local_sem.at[ch]
        )
        copy.start()
        loads.append(copy)
    own = pltpu.make_async_copy(w_in, w_buf.at[m, z, c], local_sem.at[members])
    own.start()
    tgt_copy = pltpu.make_async_copy(
        tgt_hbm.at[:, pl.ds(pl.multiple_of(m * sub, LANES), sub)], tgt, local_sem.at[members + 1]
    )
    tgt_copy.start()

    barrier = pltpu.get_barrier_semaphore()
    peers = [partner] + [z_dev(k) for k in range(1, planes)] + [member_dev(k) for k in range(1, members)]
    for dev in peers:
        pl.semaphore_signal(barrier, inc=1, device_id=dev, device_id_type=pl.DeviceIdType.MESH)
    pl.semaphore_wait(barrier, len(peers))

    z_copies = [None] + [send(w_in, w_buf.at[m, z, c], z_dev(k)) for k in range(1, planes)]
    own.wait()

    def transpose_chunk(ch):
        def body(t, carry):
            r0 = pl.multiple_of(t * TILE, TILE)
            lat_t[ch, :, pl.ds(r0, TILE)] = lat[ch, pl.ds(r0, TILE), :].T
            return carry
        lax.fori_loop(0, points // TILE, body, 0)

    rowbuf[...] = jnp.zeros_like(rowbuf)
    rowbuf[0:1, :vars_] = b_out[...]
    rowbuf[1:2, :vars_] = vw[...]
    b_col = jnp.broadcast_to(rowbuf[0:1, :], (LANES, LANES)).T[:vars_]
    v_col = jnp.broadcast_to(rowbuf[1:2, :], (LANES, LANES)).T[:vars_]
    lane_sums[...] = jnp.zeros_like(lane_sums)
    ot[...] = jnp.zeros_like(ot)
    sm[...] = jnp.zeros_like(sm)

    near = {2: [], 3: []}
    far = []
    to_part = {k: [] for k in range(members)}

    def hand_over(k, step):
        block = w_buf.at[mem(k), zed(-step), c]
        to_part[k].append(send(block, block, partner))
        return block

    def spread_block(step):
        if step > 0:
            z_copies[step].wait_recv()
        block = hand_over(0, step)
        for k in (2, 3):
            near[k].append(send(block, block, member_dev(k)))

    def relay_block(step):
        for k in (2, 3):
            near[k][step].wait_recv()
            block = hand_over(k, step)
            if step % 2 == k - 2:
                far.append(send(block, block, member_dev(5 - k)))

    def contract(k, first):
        ch = mem(k)
        for copy in to_part[k]:
            copy.wait_recv()

        def body(t, carry):
            r0 = pl.multiple_of(t * TILE, TILE)
            w = w_buf[ch].reshape(width, latent)
            before = b_in[...] if first else gp[pl.ds(r0, TILE), :]
            gp[pl.ds(r0, TILE), :] = before + dot(lat[ch, pl.ds(r0, TILE), :], w, NN)
            return carry

        lax.fori_loop(0, points // TILE, body, 0)

    for step in range(planes):
        spread_block(step)
        if step > 0:
            relay_block(step - 1)
        if step < members:
            loads[step].wait()
            transpose_chunk(step)
    for ch in range(planes, members):
        loads[ch].wait()
        transpose_chunk(ch)
    contract(0, True)
    relay_block(planes - 1)
    contract(2, False)
    contract(3, False)
    for step in range(planes):
        far[step].wait_recv()
        hand_over(1, step)
    for copy in to_part[1]:
        copy.wait_recv()

    last = mem(1)
    c0 = math.sqrt(2.0 / math.pi)
    f_copies = [None]
    for k in range(1, members + 1):
        base = mem(k) * sub

        def body(t, carry, base=base):
            r0 = pl.multiple_of(base + t * TILE, TILE)
            x = dot(lat[last, pl.ds(r0, TILE), :], w_buf[last].reshape(width, latent), NN)
            x = x + gp[pl.ds(r0, TILE), :]
            sq = x * x
            cdf = 0.5 + 0.5 * jnp.tanh(x * (c0 + (0.044715 * c0) * sq))
            out = x * cdf
            act[pl.ds(r0, TILE), :] = out.astype(BF)
            gp[pl.ds(r0, TILE), :] = cdf + (out * (1.0 - cdf)) * (2.0 * c0 + (6.0 * 0.044715 * c0) * sq)
            return carry

        lax.fori_loop(0, sub // TILE, body, 0)
        field = dot(w_out[...], act[pl.ds(pl.multiple_of(base, TILE), sub), :], NT)
        if k < members:
            fsend[k - 1] = field
            f_copies.append(send(fsend.at[k - 1], frecv.at[k], member_dev(k)))
        else:
            frecv[0] = field

    tgt_copy.wait()
    for k in range(1, members):
        f_copies[k].wait_recv()
    eps = DELTA * DELTA
    b_sum = jnp.zeros((vars_, LANES), F32)
    l_sum = jnp.zeros((vars_, LANES), F32)
    for t in range(sub // LANES):
        cols = slice(t * LANES, (t + 1) * LANES)
        place = lax.broadcasted_iota(jnp.int32, (1, LANES), 1) + (g * points + m * sub + t * LANES)
        area = jnp.cos(1.4 * (place.astype(F32) + 0.5) / total)
        scale = v_col * area
        f = [frecv[k, :, cols] for k in range(members)]
        goal = tgt[:, cols] - b_col
        pairs = [None] * members
        spread = jnp.zeros((vars_, LANES), F32)
        for a in range(members):
            for b in range(a + 1, members):
                d = f[a] - f[b]
                q = d * d + eps
                inv = lax.rsqrt(q)
                s = d * inv
                spread += q * inv - DELTA
                pairs[a] = s if pairs[a] is None else pairs[a] + s
                pairs[b] = -s if pairs[b] is None else pairs[b] - s
        miss_sum = jnp.zeros((vars_, LANES), F32)
        for a in range(members):
            d = f[a] - goal
            q = d * d + eps
            inv = lax.rsqrt(q)
            miss_sum += q * inv - DELTA
            cot = scale * (d * inv - pairs[a] * (1.0 / (members - 1)))
            b_sum += cot
            if a == 0:
                crecv[0, :, cols] = cot.astype(BF)
            else:
                csend[a - 1, :, cols] = cot.astype(BF)
        l_sum += scale * (miss_sum - spread * (1.0 / (members - 1)))
    c_copies = [None] + [send(csend.at[a - 1], crecv.at[a], member_dev(a)) for a in range(1, members)]
    lane_sums[:vars_, :] = b_sum
    sm[1:2, :LANES] = jnp.sum(lane_sums[...].T, axis=0, keepdims=True)
    sm[1:2, LANES:2 * LANES] = jnp.sum(l_sum, axis=0, keepdims=True)

    col = jnp.zeros((1, latent), F32)
    for a in range(members):
        if a > 0:
            c_copies[a].wait_recv()
        base = mem(a) * sub

        def body(t, carry, base=base, a=a):
            r0 = pl.multiple_of(base + t * TILE, TILE)
            cot_b = crecv[a, :, pl.ds(pl.multiple_of(t * TILE, TILE), TILE)]
            d = dot(cot_b, w_out[...], TN) * gp[pl.ds(r0, TILE), :]
            dpre[pl.ds(r0, TILE), :] = d.astype(BF)
            ot[:vars_, :] += dot(cot_b, act[pl.ds(r0, TILE), :], NN)
            return carry + jnp.sum(d, axis=0, keepdims=True)

        col = lax.fori_loop(0, sub // TILE, body, col)
    sm[0:1, :] = col

    share = ot.shape[0] // (2 * members)
    first_half = pl.multiple_of(other * (members * share), share)
    op_send[...] = ot[pl.ds(first_half, members * share), :].astype(BF)
    op_copy = send(op_send, op_recv, partner)
    sp_copy = send(sm, sp_recv, partner)

    def chunk(k):
        t = mem(k)
        part = dot(lat_t[t], dpre[...], NN).reshape(planes, 2, rows, latent)
        gather_ref = keep
        gather_ref[...] = part
        p_send[k - 1] = keep[:, other].astype(BF)
        m_keep_k = keep[:, c]
        return m_keep_k, send(p_send.at[k - 1], p_recv.at[k - 1], partner)

    def chip_sum(k, mine, copy):
        copy.wait_recv()
        return mine + p_recv[k - 1].astype(F32)

    def to_member(k):
        p_copies[k].wait_recv()
        m_send[k - 1] = (z_keep[k - 1] + p_recv[k - 1].astype(F32)).astype(BF)
        m_copies[k] = [
            send(m_send.at[k - 1, zed(step)], m_recv.at[k - 1, zed(step)], member_dev(k))
            for step in list(range(1, planes)) + [0]
        ]

    p_copies = {}
    m_copies = {}

    def do_chunk(k):
        z_keep[k - 1], p_copies[k] = chunk(k)

    outs = []

    def hidden_grad(ch):
        def body(t, carry):
            r0 = pl.multiple_of(t * TILE, TILE)
            w = w_buf[ch].reshape(width, latent)
            gh[ch, pl.ds(r0, TILE), :] = dot(dpre[pl.ds(r0, TILE), :], w, NT).astype(BF)
            return carry

        lax.fori_loop(0, points // TILE, body, 0)
        copy = pltpu.make_async_copy(gh.at[ch], gh_hbm.at[0, :, pl.ds(ch * width, width)], out_sem.at[ch])
        copy.start()
        outs.append(copy)

    do_chunk(1)
    do_chunk(2)
    to_member(1)
    do_chunk(3)
    to_member(2)
    op_copy.wait_recv()
    mine = pl.multiple_of(c * (members * share), share)
    om_keep[...] = (ot[pl.ds(mine, members * share), :] + op_recv[...].astype(F32)).reshape(members, share, latent)
    om_send[...] = om_keep[...].astype(BF)
    om_copies = [send(om_send.at[mem(k)], om_recv.at[k - 1], member_dev(k)) for k in range(1, members)]
    sp_copy.wait_recv()
    smm[m] = sm[...] + sp_recv[...]
    sm_copies = [send(smm.at[m], smm.at[m], member_dev(k)) for k in range(1, members)]
    do_chunk(4)
    to_member(3)
    hidden_grad(0)
    acc = om_keep[m]
    for k in range(1, members):
        om_copies[k - 1].wait_recv()
        acc += om_recv[k - 1].astype(F32)
    oz[z] = acc.astype(BF)
    oz_copies = [send(oz.at[z], oz.at[z], z_dev(k)) for k in range(1, planes)]
    for copy in sm_copies:
        copy.wait_recv()
    acc = smm[0]
    for k in range(1, members):
        acc += smm[k]
    smz[z] = acc
    sz_copies = [send(smz.at[z], smz.at[z], z_dev(k)) for k in range(1, planes)]
    hidden_grad(1)
    for copy in oz_copies:
        copy.wait_recv()
    acc = oz[0].astype(F32)
    for k in range(1, planes):
        acc += oz[k].astype(F32)
    w2[c, m] = acc
    w2_copies = [send(w2.at[c, m], w2.at[c, m], member_dev(k)) for k in range(1, members)]
    hidden_grad(2)
    p_copies[members].wait_recv()

    def plane_sum(step):
        at = zed(step)
        acc = z_keep[members - 1, at] + p_recv[members - 1, at].astype(F32)
        for k in range(1, members):
            m_copies[k][(step - 1) % planes].wait_recv()
            acc += m_recv[k - 1, at].astype(F32)
        return acc

    zz_copies = []

    def to_plane(step):
        z_send[step] = plane_sum(step).astype(BF)
        zz_copies.append(send(z_send.at[step], z_recv.at[step - 1], z_dev(step)))

    to_plane(1)
    hidden_grad(3)
    for step in range(2, planes):
        to_plane(step)
    for copy in w2_copies:
        copy.wait_recv()
    half_copy = send(w2.at[c], w2.at[c], partner)
    z_keep[members - 1, z] = plane_sum(0)

    kappa = 4.0 / math.sqrt(members * total)
    for copy in sz_copies:
        copy.wait_recv()
    acc = smz[0]
    for k in range(1, planes):
        acc += smz[k]
    acc = acc * kappa
    g_b1[...] = acc[0:1, :]
    g_b2[...] = acc[1:2, :vars_]
    g_loss[...] = jnp.sum(acc[1:2, LANES:2 * LANES], axis=1, keepdims=True) * (1.0 / (kappa * members * total * vars_))
    half_copy.wait_recv()
    g_w2[...] = w2[...].reshape(2 * members * share, latent)[:vars_] * kappa

    acc = z_keep[members - 1, z]
    for k in range(1, planes):
        zz_copies[k - 1].wait_recv()
        acc += z_recv[k - 1].astype(F32)
    g_w1[...] = acc * kappa
    for copy in started:
        copy.wait_send()
    for copy in outs:
        copy.wait()


def fast(latent, w_in, b_in, w_out, b_out, targets, var_weight, plan):
    members = lax.axis_size("member")
    grid = lax.axis_size("grid")
    planes = grid // 2
    points, width = latent.shape[1], latent.shape[2]
    rows = w_in.shape[0]
    vars_ = w_out.shape[0]
    sub = points // members
    cw = width // members
    share = 16 * pl.cdiv(vars_, 32 * members)
    n_sems = (planes - 1) * 4 + planes * 10 + (members - 1) * 5 + members + 3
    vmem = pl.BlockSpec(memory_space=pltpu.VMEM)
    hbm = pl.BlockSpec(memory_space=pl.ANY)
    V = pltpu.VMEM
    scratch = [
        V((members, points, cw), BF), V((members, cw, points), BF), V((members, planes, 2, rows, width), BF),
        V((points, width), F32), V((points, width), BF), V((points, width), BF), V((members, points, cw), BF),
        V((members - 1, vars_, sub), F32), V((members, vars_, sub), F32),
        V((members - 1, vars_, sub), BF), V((members, vars_, sub), BF), V((vars_, sub), F32),
        V((8, LANES), F32), V((LANES, LANES), F32),
        V((2 * members * share, width), F32), V((members * share, width), BF), V((members * share, width), BF),
        V((members, share, width), F32), V((members, share, width), BF), V((members - 1, share, width), BF),
        V((planes, share, width), BF), V((2, members, share, width), F32),
        V((2, width), F32), V((2, width), F32), V((members, 2, width), F32), V((planes, 2, width), F32),
        V((planes, 2, rows, width), F32), V((members, planes, rows, width), BF), V((members, planes, rows, width), BF),
        V((members - 1, planes, rows, width), BF), V((members - 1, planes, rows, width), BF),
        V((members, planes, rows, width), F32), V((planes, rows, width), BF), V((planes - 1, rows, width), BF),
        pltpu.SemaphoreType.DMA((n_sems,)), pltpu.SemaphoreType.DMA((n_sems,)),
        pltpu.SemaphoreType.DMA((members + 2,)), pltpu.SemaphoreType.DMA((members,)),
    ]
    S = jax.ShapeDtypeStruct
    gh, g_w1, g_b1, g_w2, g_b2, g_loss = pl.pallas_call(
        functools.partial(head_kernel, members, planes),
        out_shape=[
            S((1, points, width), BF), S((rows, width), F32), S((1, width), F32),
            S((vars_, width), F32), S((1, vars_), F32), S((1, 1), F32),
        ],
        in_specs=[hbm, vmem, vmem, vmem, vmem, hbm, vmem],
        out_specs=[hbm, vmem, vmem, vmem, vmem, vmem],
        scratch_shapes=scratch,
        compiler_params=pltpu.CompilerParams(
            collective_id=0, has_side_effects=True, vmem_limit_bytes=60 * 1024 * 1024
        ),
    )(latent, w_in, b_in[None], w_out, b_out[None], targets, var_weight[None])
    return g_loss[0, 0], gh, g_w1, g_b1[0], g_w2, g_b2[0]


def local(latent, w_in, b_in, w_out, b_out, targets, var_weight, plan):
    members = lax.axis_size("member")
    grid = lax.axis_size("grid")
    points, width = latent.shape[1], latent.shape[2]
    whole_plan = plan.shape[0] == members - 1
    tiled = (
        w_in.shape[0] % 16 == 0 and grid % 2 == 0 and grid >= 4 and members == 4
        and points % (members * TILE) == 0 and width % (members * LANES) == 0
        and width // members == grid * w_in.shape[0] and w_out.shape[0] <= LANES
        and points * width <= 2048 * 1024
    )
    run = fast if whole_plan and tiled else shards
    return run(latent, w_in, b_in, w_out, b_out, targets, var_weight, plan)


def solution(mesh):
    placed = (
        P("member", "grid", None),
        P(("member", "grid"), None),
        P(),
        P(),
        P(),
        P(None, "grid"),
        P(),
        P(),
    )
    return jax.shard_map(
        local,
        mesh=mesh,
        in_specs=placed,
        out_specs=(P(), P("member", "grid", None), P(("member", "grid"), None), P(), P(), P()),
        check_vma=False,
    )
```
